128 devices in a mesh: tm: 32 (over x, y, core), mp: 2 (over z_lo), dp: 2 (over z_hi).
Axes of the slice: x: 4, y: 4, z: 4 (z_hi: 2, z_lo: 2; z = z_hi * 2 + z_lo), core: 2. Of those that a mesh axis runs over, the one named last changes fastest.
Arguments:
- frames: bfloat16 [2, 4096, 1536], P('dp', 'tm'), may hold values from -12 to 12
- masked: int32 [2, 4096], P('dp', 'tm'), may hold values 0 or 1
- lengths: int32 [2], P('dp'), may hold values from 3584 to 4096
- mask_fill: bfloat16 [1536], replicated, may hold values from -4 to 4
- conv_kernel: float32 [31, 1536], replicated, may hold values from -0.6 to 0.6
- w_query: bfloat16 [1536, 1536], P(None, 'mp'), may hold values from -0.15625 to 0.15625
- w_key: bfloat16 [1536, 1536], P(None, 'mp'), may hold values from -0.15625 to 0.15625
- w_value: bfloat16 [1536, 1536], P(None, 'mp'), may hold values from -0.15625 to 0.15625
- cotangent: bfloat16 [2, 4096, 1536], P('dp', 'tm'), may hold values from -6 to 6
Outputs:
- encoded: bfloat16 [2, 4096, 1536], P('dp', 'tm', 'mp')
- grad_frames: bfloat16 [2, 4096, 1536], P('dp', 'tm')
- grad_query: float32 [1536, 1536], P(('tm', 'dp'), 'mp')
- grad_key: float32 [1536, 1536], P(('tm', 'dp'), 'mp')
- grad_value: float32 [1536, 1536], P(('tm', 'dp'), 'mp')
- grad_kernel: float32 [31, 1536], replicated
- grad_fill: float32 [1536], replicated
The draws below stay inside these ranges and needn't reach their ends.
All inputs are finite; a program needn't handle non-finite values. No bound on the sum of `masked` on one device may be relied on, other than what follows from the above.
Results may differ from the reference program's by a relative error of at most 0.015.
The reference program's roundings to bfloat16 on the way count: a program that leaves them out, or rounds other values in their place, can miss the bound.
Values may be sent and summed in bfloat16 or wider, within the bound.
No kernel may reach another device: no remote copies, remote signals or barrier semaphores. Data moves between devices by JAX's collectives and lax.ppermute only.
A program may use at most 128 MiB of HBM per device.

```python
import math
import jax
import jax.numpy as jnp
from jax import lax

D = 1536
H = 16
HEAD = 96
KERNEL = 31
BLOCK = 128
LEFT_BLOCKS = 8
TOK_DEV = 128
UTTS = 2
FRAMES = 4096


def draw_frames(key, part):
    full_shape = (UTTS, FRAMES, D)
    backdrop = jnp.clip(jax.random.normal(key, full_shape, jnp.float32), -5.0, 5.0)
    return backdrop.astype(jnp.bfloat16)


def touch_ends(values, own_key, low, top_value):
    longest = values.shape.index(max(values.shape))
    spots = []
    for shift in (0, 1):
        where = [jax.random.randint(jax.random.fold_in(own_key, axis), (), 0, length) for axis, length in enumerate(values.shape)]
        where[longest] = (where[longest] + shift) % values.shape[longest]
        spots.append(tuple(where))
    return values.at[spots[0]].set(low).at[spots[1]].set(top_value)


def shard_levels(stream_key, dims, shards, smallest, top_value):
    level = 1.0
    for dim, blocks in shards:
        steps = jax.random.uniform(jax.random.fold_in(jax.random.fold_in(stream_key, 6), dim), (blocks,), jnp.float32, smallest / len(shards), top_value / len(shards))
        level = level * jnp.repeat(jnp.exp(steps), dims[dim] // blocks).reshape((-1,) + (1,) * (len(dims) - 1 - dim))
    return level


def normal_values(own_key, extent, width, reach, cuts=(), kind=jnp.bfloat16):
    drawn = jax.random.normal(own_key, extent, jnp.float32) * width
    if len(cuts) > 0:
        drawn = shard_levels(own_key, extent, cuts, -0.22, 0.18) * drawn
    return jnp.clip(drawn, min=-reach, max=reach).astype(kind)


def setup_inputs(seed: int = 0) -> dict:
    splits = jax.random.split(jax.random.key(seed), 10)
    return {
        "frames": draw_frames(jax.random.fold_in(splits[9], 71), 0),
        "masked": touch_ends((jax.random.randint(splits[1], (UTTS, FRAMES), 0, 6) < 1).astype(jnp.int32), jax.random.fold_in(splits[1], 1), 0, 1),
        "lengths": jax.random.randint(splits[2], (UTTS,), FRAMES - 4 * TOK_DEV, FRAMES + 1).astype(jnp.int32),
        "mask_fill": normal_values(splits[3], (D,), 1.0, 4.0),
        "conv_kernel": normal_values(splits[4], (KERNEL, D), 0.1, 0.6, (), jnp.float32),
        "w_query": normal_values(splits[5], (D, D), D ** -0.5, 0.15625, ((1, 2),)),
        "w_key": normal_values(splits[6], (D, D), D ** -0.5, 0.15625, ((1, 2),)),
        "w_value": normal_values(splits[7], (D, D), D ** -0.5, 0.15625, ((1, 2),)),
        "cotangent": normal_values(splits[8], (UTTS, FRAMES, D), 1.0, 6.0, ((0, 2), (1, 32))),
    }


masked_score = -1e+30

def to_wide(value):
    return lax.optimization_barrier(value).astype(jnp.float32)

def depthwise(signal, kernel, flipped):
    frame_count = signal.shape[0]
    rim_width = (KERNEL - 1) // 2
    padded = jnp.pad(signal, ((rim_width, rim_width), (0, 0)))
    running = jnp.zeros(signal.shape, jnp.float32)
    for tap_index in range(KERNEL):
        offset = 2 * rim_width - tap_index if flipped else tap_index
        running = running + kernel[tap_index] * padded[offset:offset + frame_count]
    return running

def kernel_terms(grad, signal):
    frame_count = signal.shape[0]
    rim_width = (KERNEL - 1) // 2
    padded = jnp.pad(signal, ((rim_width, rim_width), (0, 0)))
    return jnp.stack([lax.optimization_barrier(jnp.sum(grad * padded[tap_index:tap_index + frame_count], 0)) for tap_index in range(KERNEL)])

def utterance(frames, masked, length, mask_fill, conv_kernel, w_query, w_key, w_value, cotangent):
    frame_count = frames.shape[0]
    position = jnp.arange(frame_count, dtype=jnp.int32)
    usable = position < length
    replaced = masked > 0
    x_in = jnp.where(usable[:, None], jnp.where(replaced[:, None], mask_fill[None, :], frames), jnp.zeros((), frames.dtype))
    x_wide = x_in.astype(jnp.float32)
    mixed = x_wide + depthwise(x_wide, conv_kernel, False)
    mixed_half = mixed.astype(jnp.bfloat16)
    queries = jnp.dot(mixed_half, w_query, preferred_element_type=jnp.float32).astype(jnp.bfloat16)
    key_rows = jnp.dot(mixed_half, w_key, preferred_element_type=jnp.float32).astype(jnp.bfloat16)
    value_rows = jnp.dot(mixed_half, w_value, preferred_element_type=jnp.float32).astype(jnp.bfloat16)
    span = LEFT_BLOCKS * BLOCK
    window = span + BLOCK
    block_count = frame_count // BLOCK
    head_shape = (frame_count, H, HEAD)
    score_scale = 1.0 / math.sqrt(HEAD)
    query_heads = queries.reshape(head_shape)
    key_padded = jnp.concatenate([jnp.zeros((span, H, HEAD), jnp.bfloat16), key_rows.reshape(head_shape)], 0)
    value_padded = jnp.concatenate([jnp.zeros((span, H, HEAD), jnp.bfloat16), value_rows.reshape(head_shape)], 0)

    def pieces(block_index):
        first_row = block_index * BLOCK
        query_block = lax.dynamic_slice_in_dim(query_heads, first_row, BLOCK, 0)
        key_window = lax.dynamic_slice_in_dim(key_padded, first_row, window, 0)
        value_window = lax.dynamic_slice_in_dim(value_padded, first_row, window, 0)
        key_pos = first_row - span + jnp.arange(window, dtype=jnp.int32)
        allowed = (key_pos >= 0) & (key_pos < length)
        scores = jnp.einsum('qhd,khd->hqk', query_block.astype(jnp.float32), key_window.astype(jnp.float32)) * score_scale
        scores = jnp.where(allowed[None, None, :], scores, masked_score)
        row_max = lax.optimization_barrier(jnp.max(scores, -1, keepdims=True))
        expanded = jnp.exp(scores - row_max)
        weights = expanded / lax.optimization_barrier(jnp.sum(expanded, -1, keepdims=True))
        return (query_block, key_window, value_window, weights)

    def forward_block(block_index):
        query_block, key_window, value_window, weights = pieces(block_index)
        return jnp.einsum('hqk,khd->qhd', to_wide(weights.astype(jnp.bfloat16)), value_window.astype(jnp.float32))
    block_ids = jnp.arange(block_count, dtype=jnp.int32)
    attended_heads = lax.map(forward_block, block_ids).reshape(head_shape)
    attended_wide = attended_heads.reshape(frame_count, D)
    encoded = jnp.where(usable[:, None], mixed + attended_wide, 0.0).astype(jnp.bfloat16)
    grad_in = jnp.where(usable[:, None], cotangent, jnp.zeros((), cotangent.dtype))
    grad_heads = grad_in.reshape(head_shape)

    def backward_block(running, block_index):
        key_sum, value_sum = running
        query_block, key_window, value_window, weights = pieces(block_index)
        first_row = block_index * BLOCK
        weights_half = to_wide(weights.astype(jnp.bfloat16))
        attended_block = lax.dynamic_slice_in_dim(attended_heads, first_row, BLOCK, 0)
        grad_block = lax.dynamic_slice_in_dim(grad_heads, first_row, BLOCK, 0).astype(jnp.float32)
        d_weights = jnp.einsum('qhd,khd->hqk', grad_block, value_window.astype(jnp.float32))
        row_dot = lax.optimization_barrier(jnp.sum(grad_block * attended_block, -1)).T[:, :, None]
        d_scores = to_wide((weights * (d_weights - row_dot) * score_scale).astype(jnp.bfloat16))
        query_grad = jnp.einsum('hqk,khd->qhd', d_scores, key_window.astype(jnp.float32)).astype(jnp.bfloat16)
        key_part = jnp.einsum('hqk,qhd->khd', d_scores, query_block.astype(jnp.float32))
        value_part = jnp.einsum('hqk,qhd->khd', weights_half, grad_block)
        key_sum = lax.dynamic_update_slice_in_dim(key_sum, lax.dynamic_slice_in_dim(key_sum, first_row, window, 0) + key_part, first_row, 0)
        value_sum = lax.dynamic_update_slice_in_dim(value_sum, lax.dynamic_slice_in_dim(value_sum, first_row, window, 0) + value_part, first_row, 0)
        return ((key_sum, value_sum), query_grad)
    empty = jnp.zeros((frame_count + span, H, HEAD), jnp.float32)
    (key_sum, value_sum), query_grads = lax.scan(backward_block, (empty, empty), block_ids)
    d_queries = query_grads.reshape(frame_count, D)
    key_half = key_sum[span:].reshape(frame_count, D).astype(jnp.bfloat16)
    value_half = value_sum[span:].reshape(frame_count, D).astype(jnp.bfloat16)
    grad_query = jnp.dot(mixed_half.T, d_queries, preferred_element_type=jnp.float32)
    grad_key = jnp.dot(mixed_half.T, key_half, preferred_element_type=jnp.float32)
    grad_value = jnp.dot(mixed_half.T, value_half, preferred_element_type=jnp.float32)
    mixed_grad = grad_in.astype(jnp.float32) + jnp.dot(d_queries, w_query.T, preferred_element_type=jnp.float32)
    mixed_grad = mixed_grad + jnp.dot(key_half, w_key.T, preferred_element_type=jnp.float32)
    mixed_grad = mixed_grad + jnp.dot(value_half, w_value.T, preferred_element_type=jnp.float32)
    grad_kernel = kernel_terms(mixed_grad, x_wide)
    input_grad = mixed_grad + depthwise(mixed_grad, conv_kernel, True)
    grad_frames = jnp.where((usable & ~replaced)[:, None], input_grad, 0.0).astype(jnp.bfloat16)
    grad_fill = lax.optimization_barrier(jnp.sum(jnp.where((usable & replaced)[:, None], input_grad, 0.0), 0))
    return (encoded, grad_frames, grad_query, grad_key, grad_value, grad_kernel, grad_fill)

def sum_terms(terms):
    running = terms[0]
    for extra in terms[1:]:
        running = running + extra
    return running

def reference(frames, masked, lengths, mask_fill, conv_kernel, w_query, w_key, w_value, cotangent):
    results = [utterance(frames[index], masked[index], lengths[index], mask_fill, conv_kernel, w_query, w_key, w_value, cotangent[index]) for index in range(UTTS)]
    encoded = jnp.stack([item[0] for item in results])
    grad_frames = jnp.stack([item[1] for item in results])
    summed = [sum_terms([item[slot] for item in results]) for slot in range(2, 7)]
    return (encoded, grad_frames, summed[0], summed[1], summed[2], summed[3], summed[4])
```

```python
import functools
import math

import jax
import jax.numpy as jnp
from jax import lax
from jax.experimental import pallas as pl
from jax.experimental.pallas import tpu as pltpu
from jax.sharding import Mesh
from jax.sharding import PartitionSpec as P

HEAD = 96
BLOCK = 128
LEFT_BLOCKS = 8
GROUP = 8
TAPS = 31
RIM = 15

F32 = jnp.float32
BF16 = jnp.bfloat16
masked_score = -1e30
TM = ("tx", "ty")


def dot(left, right, left_dim, right_dim):
    return lax.dot_general(
        left, right, (((left_dim,), (right_dim,)), ((), ())), preferred_element_type=F32
    )


def attention_kernel(info_ref, kv_ref, qg_ref, prev_ref, dq_ref, own_ref, back_ref, kt, vt, kn, vn, kacc, vacc):
    span = GROUP * BLOCK
    window = span + BLOCK
    scale = 1.0 / math.sqrt(HEAD)
    first_key = info_ref[0]
    length = info_ref[1]
    for part in range(2 * GROUP):
        block = prev_ref[part] if part < GROUP else kv_ref[part - GROUP]
        cols = slice(part * BLOCK, (part + 1) * BLOCK)
        kt[:, cols] = block[:HEAD]
        vt[:, cols] = block[HEAD:]
        kn[cols, :] = block[:HEAD].T
        vn[cols, :] = block[HEAD:].T
    kacc[...] = jnp.zeros_like(kacc)
    vacc[...] = jnp.zeros_like(vacc)

    def query_block(index, carry):
        start = pl.multiple_of(index * BLOCK, BLOCK)
        rows = pl.ds(start, window)
        qg = qg_ref[index]
        query_t = qg[:HEAD]
        grad_t = qg[HEAD:]
        scores = dot(kn[rows, :], query_t, 1, 0) * scale
        position = first_key + start + lax.broadcasted_iota(jnp.int32, (window, BLOCK), 0)
        allowed = (position >= 0) & (position < length)
        scores = jnp.where(allowed, scores, masked_score)
        expanded = jnp.exp(scores - jnp.max(scores, 0, keepdims=True))
        weights = expanded * (1.0 / jnp.sum(expanded, 0, keepdims=True))
        weights_half = weights.astype(BF16)
        attended = dot(vt[:, rows], weights_half, 1, 0)
        d_weights = dot(vn[rows, :], grad_t, 1, 0)
        row_dot = jnp.sum(grad_t.astype(F32) * attended, 0, keepdims=True)
        d_scores = (weights * (d_weights - row_dot) * scale).astype(BF16)
        dq_ref[index, :HEAD] = dot(kt[:, rows], d_scores, 1, 0).astype(BF16)
        dq_ref[index, HEAD:] = attended.astype(BF16)
        kacc[rows, :] += dot(d_scores, query_t, 1, 1)
        vacc[rows, :] += dot(weights_half, grad_t, 1, 1)
        return carry

    lax.fori_loop(0, GROUP, query_block, 0)
    for part in range(GROUP):
        cols = slice(part * BLOCK, (part + 1) * BLOCK)
        back_ref[part, :HEAD] = kacc[cols, :].T.astype(BF16)
        back_ref[part, HEAD:] = vacc[cols, :].T.astype(BF16)
        cols = slice(span + part * BLOCK, span + (part + 1) * BLOCK)
        own_ref[part, :HEAD] = kacc[cols, :].T
        own_ref[part, HEAD:] = vacc[cols, :].T


def attention(info, kv, qg, prev):
    pair = (GROUP, 2 * HEAD, BLOCK)
    context = 2 * GROUP * BLOCK
    vmem = pl.BlockSpec(memory_space=pltpu.VMEM)
    return pl.pallas_call(
        attention_kernel,
        out_shape=(
            jax.ShapeDtypeStruct(pair, BF16),
            jax.ShapeDtypeStruct(pair, F32),
            jax.ShapeDtypeStruct(pair, BF16),
        ),
        in_specs=[pl.BlockSpec(memory_space=pltpu.SMEM), vmem, vmem, vmem],
        out_specs=(vmem, vmem, vmem),
        scratch_shapes=[
            pltpu.VMEM((HEAD, context), BF16),
            pltpu.VMEM((HEAD, context), BF16),
            pltpu.VMEM((context, HEAD), BF16),
            pltpu.VMEM((context, HEAD), BF16),
            pltpu.VMEM((context, HEAD), F32),
            pltpu.VMEM((context, HEAD), F32),
        ],
        compiler_params=pltpu.CompilerParams(vmem_limit_bytes=32 * 1024 * 1024),
        name="attention",
    )(info, kv, qg, prev)


def halo(cells, width):
    count = lax.axis_size("tx") * lax.axis_size("ty")
    before = lax.ppermute(cells[-width:], TM, [(i, i + 1) for i in range(count - 1)])
    after = lax.ppermute(cells[:width], TM, [(i + 1, i) for i in range(count - 1)])
    return before, after


def convolve(padded, kernel, frame_count, flipped):
    running = jnp.zeros((frame_count, padded.shape[1]), F32)
    for tap in range(TAPS):
        offset = 2 * RIM - tap if flipped else tap
        running = running + kernel[tap] * padded[offset : offset + frame_count].astype(F32)
    return running


def gathered(rows):
    half = GROUP // 2
    up = [(2 * y + c, 2 * ((y + 1) % half) + c) for y in range(half) for c in range(2)]
    down = [(b, a) for a, b in up]
    turn = [up[2 * y] for y in range(half)] + [down[2 * y + 1] for y in range(half)]
    swap = [(2 * y + c, 2 * y + 1 - c) for y in range(half) for c in range(2)]
    from_below = lax.ppermute(rows, "ty", up)
    from_above = lax.ppermute(rows, "ty", down)
    core = lax.axis_index("ty") % 2
    far = lax.ppermute(jnp.where(core == 0, from_below, from_above), "ty", turn)
    mine = jnp.concatenate([rows, from_below, from_above, far], 0)
    other = lax.ppermute(mine, "ty", swap)
    chip = lax.axis_index("ty") // 2
    chips = jnp.stack([chip, (chip + half - 1) % half, (chip + 1) % half, (chip + 2) % half])
    order = jnp.concatenate([chips * 2 + core, chips * 2 + 1 - core])
    return mine, other, order


def on_device(frames, masked, lengths, mask_fill, conv_kernel, w_query, w_key, w_value, cotangent):
    frame_count, width = frames.shape[1:]
    half = w_query.shape[1]
    groups = lax.axis_size("tx")
    group = lax.axis_index("tx")
    part = lax.axis_index("mp")
    first_frame = (group * GROUP + lax.axis_index("ty")) * frame_count
    first_column = part * half
    length = lengths[0]
    usable = (first_frame + jnp.arange(frame_count, dtype=jnp.int32)) < length
    replaced = masked[0] > 0
    zero_half = jnp.zeros((), BF16)
    x_in = jnp.where(
        usable[:, None], jnp.where(replaced[:, None], mask_fill[None, :], frames[0]), zero_half
    )
    x_before, x_after = halo(x_in, RIM)
    x_padded = jnp.concatenate([x_before, x_in, x_after], 0)
    mixed = x_in.astype(F32) + convolve(x_padded, conv_kernel, frame_count, False)
    mixed_half = mixed.astype(BF16)

    def half_columns(array):
        return lax.dynamic_slice_in_dim(array, first_column, half, 1)

    def per_head(array):
        return array.astype(BF16).reshape(GROUP, HEAD, frame_count)

    grad_in = jnp.where(usable[:, None], half_columns(cotangent[0]), zero_half)
    kv = jnp.concatenate(
        [per_head(dot(w_key, mixed_half, 0, 1)), per_head(dot(w_value, mixed_half, 0, 1))], 1
    )
    qg = jnp.concatenate([per_head(dot(w_query, mixed_half, 0, 1)), per_head(grad_in.T)], 1)
    kv = lax.all_to_all(kv, "ty", 0, 0, tiled=True)
    prev = lax.ppermute(kv, "tx", [(i, i + 1) for i in range(groups - 1)])
    qg = lax.all_to_all(qg, "ty", 0, 0, tiled=True)
    info = jnp.stack([(group - 1) * GROUP * frame_count, length]).astype(jnp.int32)
    dq, own, back = attention(info, kv, qg, prev)

    late = lax.ppermute(back, "tx", [(i + 1, i) for i in range(groups - 1)])
    dq_rows = lax.all_to_all(dq, "ty", 0, 0, tiled=True)
    d_kv = (own + late.astype(F32)).astype(BF16)
    kv_rows = lax.all_to_all(d_kv, "ty", 0, 0, tiled=True)
    d_query = dq_rows[:, :HEAD].reshape(half, frame_count)
    attended = dq_rows[:, HEAD:].reshape(half, frame_count).T.astype(F32)
    d_key = kv_rows[:, :HEAD].reshape(half, frame_count)
    d_value = kv_rows[:, HEAD:].reshape(half, frame_count)
    encoded = jnp.where(usable[:, None], half_columns(mixed) + attended, 0.0).astype(BF16)

    back_mix = dot(d_query, w_query, 0, 1) + dot(d_key, w_key, 0, 1) + dot(d_value, w_value, 0, 1)
    swap = [(0, 1), (1, 0)]
    theirs = lax.dynamic_slice_in_dim(back_mix, half - first_column, half, 1).astype(BF16)
    theirs = lax.ppermute(theirs, "mp", swap)
    mixed_grad = grad_in.astype(F32) + half_columns(back_mix) + theirs.astype(F32)
    grad_before, grad_after = halo(mixed_grad, RIM)
    grad_padded = jnp.concatenate([grad_before, mixed_grad, grad_after], 0)
    input_grad = mixed_grad + convolve(
        grad_padded, half_columns(conv_kernel), frame_count, True
    )
    x_half = half_columns(x_padded)
    fill_part = jnp.sum(jnp.where((usable & replaced)[:, None], input_grad, 0.0), 0)
    kernel_part = jnp.stack(
        [
            jnp.sum(mixed_grad * x_half[tap : tap + frame_count].astype(F32), 0)
            for tap in range(TAPS)
        ]
        + [fill_part]
    )
    grad_half = jnp.where((usable & ~replaced)[:, None], input_grad, 0.0).astype(BF16)
    grad_other = lax.ppermute(grad_half, "mp", swap)
    low = jnp.where(part == 0, grad_half, grad_other)
    high = jnp.where(part == 0, grad_other, grad_half)
    grad_frames = jnp.concatenate([low, high], 1)

    mine, other, order = gathered(mixed_half)
    d_all = jnp.concatenate([dq[:, :HEAD], d_kv], 1)
    picked = jnp.take(d_all, order, axis=0, unique_indices=True, mode="clip")
    picked = picked.transpose(1, 0, 2).reshape(3 * HEAD, GROUP * frame_count)
    weight_grad = dot(mine, picked[:, : GROUP // 2 * frame_count], 0, 1) + dot(
        other, picked[:, GROUP // 2 * frame_count :], 0, 1
    )
    everyone = ("tx", "ty", "dp")
    count = groups * GROUP * lax.axis_size("dp")
    rows = width // count
    terms = weight_grad.astype(BF16).reshape(count, rows, 3 * HEAD)
    spare = 2 * 3 * HEAD - TAPS_ROWS * half // count
    taps = kernel_part.reshape(count, TAPS_ROWS * half // count).astype(BF16)
    taps = jnp.pad(taps, ((0, 0), (0, spare))).reshape(count, 2, 3 * HEAD)
    terms = lax.all_to_all(jnp.concatenate([terms, taps], 1), everyone, 0, 0, tiled=True)
    terms = terms.reshape(groups, GROUP, 2, rows + 2, 3 * HEAD).astype(F32)
    weight_sum = jnp.sum(terms[:, :, :, :rows], (0, 2))
    tap_sum = jnp.sum(terms[:, :, :, rows:], (0, 1, 2)).reshape(-1)[: TAPS_ROWS * half // count]
    weight_sum = weight_sum.transpose(1, 0, 2)
    grads = [
        weight_sum[:, :, i * HEAD : (i + 1) * HEAD].reshape(rows, half) for i in range(3)
    ]
    taps = jnp.broadcast_to(tap_sum[None], (2 * count, tap_sum.shape[0]))
    taps = lax.all_to_all(taps, ("mp", "tx", "ty", "dp"), 0, 0, tiled=True)
    taps = taps.reshape(2, TAPS_ROWS, half).transpose(1, 0, 2).reshape(TAPS_ROWS, width)
    return (encoded[None], grad_frames[None], *grads, taps[:TAPS], taps[TAPS])


TAPS_ROWS = TAPS + 1


def solution(mesh):
    tm, mp, dp = (mesh.shape[name] for name in ("tm", "mp", "dp"))
    devices = mesh.devices.reshape(tm // GROUP, GROUP, mp, dp)
    mesh = Mesh(devices, ("tx", "ty", "mp", "dp"))
    in_specs = (
        P("dp", TM, None),
        P("dp", TM),
        P("dp"),
        P(),
        P(),
        P(None, "mp"),
        P(None, "mp"),
        P(None, "mp"),
        P("dp", TM, None),
    )
    out_specs = (
        P("dp", TM, "mp"),
        P("dp", TM, None),
        P(("tx", "ty", "dp"), "mp"),
        P(("tx", "ty", "dp"), "mp"),
        P(("tx", "ty", "dp"), "mp"),
        P(),
        P(),
    )
    return jax.shard_map(
        on_device, mesh=mesh, in_specs=in_specs, out_specs=out_specs, check_vma=False
    )
```
